512 devices in a mesh: chain: 2 (over x_lo), slab: 128 (over x_hi, z, y), vis: 2 (over core).
Axes of the slice: x: 4 (x_hi: 2, x_lo: 2; x = x_hi * 2 + x_lo), y: 8, z: 8, core: 2. Of those that a mesh axis runs over, the one named last changes fastest.
Arguments:
- screens: float32 [4, 2048, 2048], P(('chain', 'vis'), 'slab'), parts along dimension 0, may hold values from -6 to 6
- image: float32 [4096, 2048], P(('chain', 'slab')), parts along dimension 0, may hold values from -6 to 6
- vis_row: int32 [32768], P('slab'), may hold values from 0 to 2047
- vis_block: int32 [32768, 1], P('slab'), may hold values from 0 to 127; in each aligned block of 256 rows (0 to 255, 256 to 511, ...) at most 6 rows name the same one
- vis_column: int32 [32768], P('slab'), may hold values from 0 to 7
- vis_real: float32 [32768], P('slab'), may hold values from -6 to 6
- vis_imag: float32 [32768], P('slab'), may hold values from -6 to 6
- vis_weight: float32 [32768], P('slab'), may hold values from 0.5 to 4
Outputs:
- screen_grad: float32 [4, 2048, 2048], P(('chain', 'vis'), 'slab'), parts along dimension 0
The draws below stay inside these ranges and needn't reach their ends.
There are 2 independent parts, one for each index of `chain`. The reference program is written for one: setup_inputs(seed, part) draws one part's arguments, and reference() takes and returns one part's arrays. A program takes and returns all parts, laid end to end along the dimension named above; an argument that names none is the same for every part. Nothing has to cross between parts.
Inputs may be any that keep to these rules, and one draw needn't show every extreme that they name: `vis_block`: among the 256 visibilities of one index of slab, at most 6 name any one block; in every draw some block of some index holds exactly 6.
All inputs are finite; a program needn't handle non-finite values.
Results may differ from the reference program's by a relative error of at most 0.013.
Values may be sent and summed in bfloat16 or wider, within the bound.
No kernel may reach another device: no remote copies, remote signals or barrier semaphores. Data moves between devices by JAX's collectives and lax.ppermute only.
A program may use at most 64 MiB of HBM per device.

```python
import math
import jax
import jax.numpy as jnp
import numpy as np
from jax import lax

GRID = 2048
VIS_DEV = 256
WALK = 2
VIS = 32768
KX_BLOCK = 8
CAP = 6
N_SLAB = 128


def plant(values, own_key, smallest, largest):
    longest = values.shape.index(max(values.shape))
    spots = []
    for shift in (0, 1):
        where = [jax.random.randint(jax.random.fold_in(own_key, axis), (), 0, length) for axis, length in enumerate(values.shape)]
        where[longest] = (where[longest] + shift) % values.shape[longest]
        spots.append(tuple(where))
    return values.at[spots[0]].set(smallest).at[spots[1]].set(largest)


def block_levels(own_key, extent, cuts, low, top_value):
    gain = 1.0
    for position, parts in cuts:
        draws = jax.random.uniform(jax.random.fold_in(jax.random.fold_in(own_key, 6), position), (parts,), jnp.float32, low / len(cuts), top_value / len(cuts))
        gain = gain * jnp.repeat(jnp.exp(draws), extent[position] // parts).reshape((-1,) + (1,) * (len(extent) - 1 - position))
    return gain


def deal_out(own_key, own, number, rows, amount, top, reach, lean):
    order = jax.random.permutation(own_key, amount)
    heavy_load, ordinary = portions_of(amount, rows * top, reach, lean, True), portions_of(amount, rows * top, reach, lean, False)
    places = jnp.arange(amount)

    def named(sizes, offset_by):
        used = int((sizes > 0).sum())
        fixed = max(1, used // 4)
        passed = fixed + (places - fixed + offset_by * (used - fixed)) % max(1, amount - fixed)
        return jnp.zeros((amount,), jnp.int32).at[order[jnp.where(places < fixed, places, passed)]].set(jnp.asarray(sizes, jnp.int32))

    sizes = jnp.where(number % 4 == 0, named(heavy_load, number // 4), named(ordinary, number - number // 4 - 1))
    mixed = jax.random.permutation(jax.random.fold_in(own, 3), amount)
    giver, sink = mixed[0:amount // 2 * 2:2], mixed[1:amount // 2 * 2:2]
    slack = jnp.minimum(sizes[giver] - 1, reach - sizes[sink]) // 2
    slack = jnp.where((giver == order[0]) | (sink == order[0]) | (sizes[sink] == 0), 0, jnp.maximum(slack, 0))
    passed = jax.random.randint(jax.random.fold_in(own, 4), (amount // 2,), 0, 1 << 20) % (slack + 1)
    sizes = sizes.at[giver].add(-passed).at[sink].add(passed)
    items = jnp.searchsorted(jnp.cumsum(sizes), jnp.arange(rows * top), side="right").astype(jnp.int32)
    table = items.reshape(top, rows).T
    table = table[jax.random.permutation(jax.random.fold_in(own, 1), rows)]
    offset_by = jax.random.randint(jax.random.fold_in(own, 2), (rows, 1), 0, top)
    return jnp.take_along_axis(table, (jnp.arange(top)[None, :] + offset_by) % top, axis=1)


def portions_of(number_of, total, limit, lean, full):
    portions = [(1 << 20) // math.isqrt(standing ** lean) + 1 for standing in range(1, number_of + 1)]
    largest = limit if full else min(limit, max(-(-total // number_of), total * portions[0] // sum(portions)))
    least = 1 if total - largest >= number_of - 1 else 0
    holding, surplus = [largest] + [least] * (number_of - 1), total - largest - least * (number_of - 1)
    while surplus > 0:
        movable = [i for i in range(1, number_of) if holding[i] < largest] or [i for i in range(1, number_of) if holding[i] < limit]
        pool, budget = sum([portions[i] for i in movable]), surplus
        for i in movable:
            extra = min(limit - holding[i], max(1, budget * portions[i] // pool), surplus)
            holding[i] = holding[i] + extra
            surplus = surplus - extra
    return np.array(holding)


def gaussian(rng, shape, width, most, cuts=(), kind=jnp.bfloat16):
    drawn = jax.random.normal(rng, shape, jnp.float32) * width
    if len(cuts) > 0:
        drawn = block_levels(rng, shape, cuts, -0.22, 0.18) * drawn
    return jnp.clip(drawn, min=-most, max=most).astype(kind)


def setup_inputs(seed: int = 0, part: int = 0) -> dict:
    splits = jax.random.split(jax.random.key(seed), 9)
    part_splits = jax.random.split(jax.random.fold_in(splits[8], part), 9)
    screens = gaussian(part_splits[0], (WALK, GRID, GRID), 1.0, 6.0, ((0, 2), (1, 128)), jnp.float32)
    image = gaussian(part_splits[1], (GRID, GRID), 1.0, 6.0, ((0, 128),), jnp.float32)
    vis_row = plant(jax.random.randint(splits[2], (VIS,), 0, GRID), jax.random.fold_in(splits[2], 1), 0, GRID - 1).astype(jnp.int32)
    vis_block_keys = jax.random.split(jax.random.fold_in(splits[3], 1), VIS // VIS_DEV)
    vis_block_turns = jax.random.permutation(jax.random.fold_in(splits[3], 3), VIS // VIS_DEV)
    vis_block = jax.vmap(lambda own, number: deal_out(jax.random.fold_in(splits[3], 2), own, number, VIS_DEV, N_SLAB, 1, CAP, 2))(vis_block_keys, vis_block_turns).reshape((VIS, 1))
    vis_column = plant(jax.random.randint(splits[4], (VIS,), 0, KX_BLOCK), jax.random.fold_in(splits[4], 1), 0, KX_BLOCK - 1).astype(jnp.int32)
    vis_real = gaussian(splits[5], (VIS,), 1.0, 6.0, ((0, 128),), jnp.float32)
    vis_imag = gaussian(splits[6], (VIS,), 1.0, 6.0, ((0, 128),), jnp.float32)
    vis_weight = jnp.clip(jnp.exp(math.log(4.0) - 2.0794415 * jax.random.uniform(splits[7], (VIS,), jnp.float32) ** block_levels(splits[7], (VIS,), ((0, 128),), -0.2, 0.2)), 0.5, 4.0)
    return {"screens": screens, "image": image, "vis_row": vis_row, "vis_block": vis_block, "vis_column": vis_column, "vis_real": vis_real, "vis_imag": vis_imag, "vis_weight": vis_weight}


refract = 1.0

def twiddle(first, second, length):
    phase = (first[:, None] * second[None, :] % length).astype(jnp.float32) * (2.0 * math.pi / length)
    return (jnp.cos(phase).astype(jnp.bfloat16), jnp.sin(phase).astype(jnp.bfloat16))

def col_slope(field):
    return (8.0 * (jnp.roll(field, -1, -1) - jnp.roll(field, 1, -1)) - (jnp.roll(field, -2, -1) - jnp.roll(field, 2, -1))) / 12.0

def col_adjoint(field):
    return (8.0 * (jnp.roll(field, 1, -1) - jnp.roll(field, -1, -1)) - (jnp.roll(field, 2, -1) - jnp.roll(field, -2, -1))) / 12.0

def row_slope(field):
    return (8.0 * (jnp.roll(field, -1, -2) - jnp.roll(field, 1, -2)) - (jnp.roll(field, -2, -2) - jnp.roll(field, 2, -2))) / 12.0

def row_adjoint(field):
    return (8.0 * (jnp.roll(field, 1, -2) - jnp.roll(field, -1, -2)) - (jnp.roll(field, 2, -2) - jnp.roll(field, -2, -2))) / 12.0

def reference(screens, image, vis_row, vis_block, vis_column, vis_real, vis_imag, vis_weight):
    unitary = 1.0 / math.sqrt(GRID)
    half_kx = GRID // 2
    positions = jnp.arange(GRID, dtype=jnp.int32)
    cos_half, sin_half = twiddle(jnp.arange(half_kx, dtype=jnp.int32), positions, GRID)
    image_x = col_slope(image)
    image_y = row_slope(image)
    joined = (image[None] + refract * (col_slope(screens) * image_x[None] + row_slope(screens) * image_y[None])).astype(jnp.bfloat16)
    flat = joined.reshape(WALK * GRID, GRID)
    spec_real = (unitary * jnp.dot(flat, cos_half.T, preferred_element_type=jnp.float32)).astype(jnp.bfloat16)
    spec_imag = (-unitary * jnp.dot(flat, sin_half.T, preferred_element_type=jnp.float32)).astype(jnp.bfloat16)
    trans_real = jnp.transpose(spec_real.reshape(WALK, GRID, half_kx), (0, 2, 1))
    trans_imag = jnp.transpose(spec_imag.reshape(WALK, GRID, half_kx), (0, 2, 1))
    col_index = (vis_block[:, 0] * KX_BLOCK + vis_column).astype(jnp.int32)
    step_size = math.gcd(2048, VIS)
    steps_count = VIS // step_size

    def visit(sums, inputs):
        row_freq, col_freq, real_part, imag_part, weight = inputs
        cos_rows, sin_rows = twiddle(row_freq, positions, GRID)
        cos_full = cos_rows.astype(jnp.float32)[None]
        sin_full = sin_rows.astype(jnp.float32)[None]
        pick_real = trans_real[:, col_freq, :].astype(jnp.float32)
        pick_imag = trans_imag[:, col_freq, :].astype(jnp.float32)
        model_real = unitary * lax.optimization_barrier(jnp.sum(cos_full * pick_real + sin_full * pick_imag, -1))
        model_imag = unitary * lax.optimization_barrier(jnp.sum(cos_full * pick_imag - sin_full * pick_real, -1))
        error_real = lax.optimization_barrier((weight[None] * (model_real - real_part[None])).astype(jnp.bfloat16)).astype(jnp.float32)
        error_imag = lax.optimization_barrier((weight[None] * (model_imag - imag_part[None])).astype(jnp.bfloat16)).astype(jnp.float32)
        term_real = cos_full * error_real[:, :, None] - sin_full * error_imag[:, :, None]
        term_imag = sin_full * error_real[:, :, None] + cos_full * error_imag[:, :, None]
        return ((sums[0].at[:, col_freq, :].add(term_real), sums[1].at[:, col_freq, :].add(term_imag)), None)
    zeros_grid = jnp.zeros((WALK, half_kx, GRID), jnp.float32)
    inputs = (vis_row.astype(jnp.int32).reshape(steps_count, step_size), col_index.reshape(steps_count, step_size), vis_real.reshape(steps_count, step_size), vis_imag.reshape(steps_count, step_size), vis_weight.reshape(steps_count, step_size))
    (sum_real, sum_imag), _ = lax.scan(visit, (zeros_grid, zeros_grid), inputs)
    back_real = (unitary * sum_real).astype(jnp.bfloat16)
    back_imag = (unitary * sum_imag).astype(jnp.bfloat16)
    rows_real = jnp.transpose(back_real, (0, 2, 1)).reshape(WALK * GRID, half_kx)
    rows_imag = jnp.transpose(back_imag, (0, 2, 1)).reshape(WALK * GRID, half_kx)
    gradient = jnp.dot(rows_real, cos_half, preferred_element_type=jnp.float32) - jnp.dot(rows_imag, sin_half, preferred_element_type=jnp.float32)
    gradient = (unitary * gradient).reshape(WALK, GRID, GRID)
    push_x = refract * image_x[None] * gradient
    push_y = refract * image_y[None] * gradient
    return col_adjoint(push_x) + row_adjoint(push_y)
```

```python
import functools
import math

import jax
import jax.numpy as jnp
import numpy as np
from jax import lax
from jax.experimental import pallas as pl
from jax.experimental.pallas import tpu as pltpu
from jax.sharding import PartitionSpec as P

INTERPRET = False
F32 = jnp.float32
BF16 = jnp.bfloat16

GRID = 2048
ROWS = 16
SLABS = 128
OWNED = 8
CAP = 6
SLOTS = 8
FIELDS = 8
UNITARY = 1.0 / math.sqrt(GRID)
NT = (((1,), (1,)), ((), ()))


def wave(first, second, length):
    phase = (np.arange(first)[:, None] * np.arange(second)[None, :] % length) * (2.0 * np.pi / length)
    return np.cos(phase), np.sin(phase)


@functools.lru_cache(None)
def tables():
    out = {}
    cos, sin = wave(64, 128, 128)
    wide = np.zeros((2, 64, 2, 2, 2, 128))
    for half in range(2):
        wide[0, :, half, half, 0] = cos
        wide[0, :, half, half, 1] = sin
        wide[1, :, half, half, 0] = -sin
        wide[1, :, half, half, 1] = cos
    out["row_mix"] = (UNITARY * wide.reshape(256, 512), BF16)
    cos, sin = wave(16, 128, GRID)
    out["row_turn"] = (np.concatenate([cos, sin], 0), F32)
    cos, sin = wave(128, 128, 128)
    mix = UNITARY * np.block([[cos, sin], [-sin, cos]])
    out["col_mix"] = (mix, BF16)
    out["col_mix_back"] = (mix.T, BF16)
    cos, sin = wave(128, 16, GRID)
    out["col_turn"] = (np.concatenate([np.tile(cos, (1, 8)), np.tile(sin, (1, 8))], 1), F32)
    cos, sin = wave(16, 16, 16)
    cos, sin = np.kron(np.eye(8), cos), np.kron(np.eye(8), sin)
    mix = np.block([[cos, -sin], [sin, cos]])
    out["fine_mix"] = (mix, BF16)
    out["fine_mix_back"] = (mix.T, BF16)
    cos, sin = wave(256, 128, 256)
    out["out_mix"] = (UNITARY * np.block([[cos, -sin], [sin, cos]]), BF16)
    cos, sin = wave(256, 8, GRID)
    out["out_turn"] = (np.concatenate([np.repeat(cos, 16, 1), np.repeat(sin, 16, 1)], 1), F32)
    cos, sin = wave(8, 8, 8)
    out["out_fine"] = (np.concatenate([np.kron(cos, np.eye(16)), -np.kron(sin, np.eye(16))], 1), BF16)
    return out


def table(name):
    values, kind = tables()[name]
    return jnp.asarray(values.astype(np.float32)).astype(kind)


def roll(field, shift, axis):
    return pltpu.roll(field, shift % field.shape[axis], axis)


def col_slope(field):
    return (8.0 / 12.0) * (roll(field, -1, 1) - roll(field, 1, 1)) - (1.0 / 12.0) * (
        roll(field, -2, 1) - roll(field, 2, 1)
    )


def row_slope(ref, count):
    return (8.0 / 12.0) * (ref[3 : count + 3, :] - ref[1 : count + 1, :]) - (1.0 / 12.0) * (
        ref[4 : count + 4, :] - ref[0:count, :]
    )


def bucket_kernel(cells, bucket):
    data = cells[...]
    count = data.shape[1]
    block = data[1:2, :]
    hot = (lax.broadcasted_iota(jnp.int32, (SLABS, count), 0).astype(F32) == block).astype(F32)
    earlier = (
        lax.broadcasted_iota(jnp.int32, (count, count), 0)
        < lax.broadcasted_iota(jnp.int32, (count, count), 1)
    ).astype(F32).astype(BF16)
    before = jnp.dot(hot.astype(BF16), earlier, preferred_element_type=F32)
    rank = jnp.sum(before * hot, 0, keepdims=True)
    row = data[0:1, :]
    row_high = jnp.floor(row * (1.0 / 128.0))
    weight = data[5:6, :]
    fields = [row - 128.0 * row_high, data[2:3, :] * 16.0 + row_high]
    for value in (weight, weight * data[3:4, :], weight * data[4:5, :]):
        high = value.astype(BF16).astype(F32)
        fields += [high, value - high]
    slot = lax.broadcasted_iota(jnp.int32, (SLOTS, count), 0).astype(F32)
    mine = slot == rank
    spread = jnp.concatenate([jnp.where(mine, field, 0.0) for field in fields], 0)
    filled = lax.dot_general(hot.astype(BF16), spread.astype(BF16), NT, preferred_element_type=F32)
    bucket[...] = jnp.concatenate([filled, jnp.zeros_like(filled)], 1)


def forward_kernel(screen, image, above, below, bucket, mix, turn, message, image_x, image_y, pad_image, pad_screen, mixed):
    top = above[...].astype(F32)
    low = below[...].astype(F32)
    own_screen = screen[0]
    own_image = image[...]
    pad_image[0:4, :] = top[0:4]
    pad_image[4:20, :] = own_image
    pad_image[20:24, :] = low[0:4]
    pad_screen[0:2, :] = top[4:6]
    pad_screen[2:18, :] = own_screen
    pad_screen[18:20, :] = low[4:6]
    image_y[0:20, :] = row_slope(pad_image, 20)
    slope_x = col_slope(own_image)
    image_x[...] = slope_x
    joined = own_image + col_slope(own_screen) * slope_x + row_slope(pad_screen, 16) * image_y[2:18, :]
    joined = joined.astype(BF16).astype(F32)
    part = [joined[:, 128 * i : 128 * (i + 1)] for i in range(16)]
    even = [part[i] + part[16 - i] for i in range(1, 8)]
    odd = [part[i] - part[16 - i] for i in range(1, 8)]
    for k in range(9):
        real = part[0] + part[8] if k % 2 == 0 else part[0] - part[8]
        imag = jnp.zeros_like(real)
        for i in range(1, 8):
            angle = 2.0 * math.pi * ((i * k) % 16) / 16.0
            real = real + math.cos(angle) * even[i - 1]
            if (i * k) % 8 != 0:
                imag = imag - math.sin(angle) * odd[i - 1]
        for target in {k, (16 - k) % 16}:
            sign = 1.0 if target == k else -1.0
            cos = turn[target : target + 1, :]
            sin = turn[16 + target : 17 + target, :]
            half, fine = divmod(target, 8)
            rows = slice(16 * fine, 16 * fine + 16)
            mixed[rows, 256 * half : 256 * half + 128] = (real * cos + (sign * imag) * sin).astype(BF16)
            mixed[rows, 256 * half + 128 : 256 * half + 256] = ((sign * imag) * cos - real * sin).astype(BF16)
    spectra = lax.dot_general(mix[...], mixed[...], NT, preferred_element_type=F32)
    message[:, 0, :] = spectra[0:128]
    message[:, 1, :] = spectra[128:256]
    message[:, 2, :] = bucket[...]


def middle_kernel(arrived, mix, turn, fine, fine_back, mix_back, message):
    cells = jnp.transpose(arrived[:, 2, :])
    total = SLABS * CAP
    index = lax.broadcasted_iota(jnp.int32, (128, total), 0).astype(F32)

    def line(field):
        return jnp.concatenate([cells[SLOTS * field + s : SLOTS * field + s + 1, :] for s in range(CAP)], 1)

    row_hot = (index == line(0)).astype(F32).astype(BF16)
    chosen = index == line(1)
    spread = jnp.concatenate(
        [jnp.where(chosen, line(2 + t), 0.0).astype(BF16) for t in range(6)], 0
    )
    sums = lax.dot_general(row_hot, spread, NT, preferred_element_type=F32)
    weight = sums[:, 0:128] + sums[:, 128:256]
    seen_real = sums[:, 256:384] + sums[:, 384:512]
    seen_imag = sums[:, 512:640] + sums[:, 640:768]
    cos = turn[:, 0:128]
    sin = turn[:, 128:256]
    spectra = jnp.concatenate([arrived[:, 0, :], arrived[:, 1, :]], 0).astype(BF16)
    coarse = jnp.dot(mix[...], spectra, preferred_element_type=F32)
    real, imag = coarse[0:128], coarse[128:256]
    turned = jnp.concatenate([real * cos + imag * sin, imag * cos - real * sin], 1).astype(BF16)
    model = jnp.dot(turned, fine[...], preferred_element_type=F32)
    error = jnp.concatenate(
        [weight * model[:, 0:128] - seen_real, weight * model[:, 128:256] - seen_imag], 1
    ).astype(BF16)
    spread_back = jnp.dot(error, fine_back[...], preferred_element_type=F32)
    real, imag = spread_back[:, 0:128], spread_back[:, 128:256]
    turned = jnp.concatenate([real * cos - imag * sin, imag * cos + real * sin], 0).astype(BF16)
    back = jnp.dot(mix_back[...], turned, preferred_element_type=F32)
    back_real, back_imag = back[0:128], back[128:256]
    row = lax.broadcasted_iota(jnp.int32, (128, 128), 1) % ROWS
    first = row < 2
    real_side = jnp.where(first, roll(back_real, -1, 0), roll(back_real, 1, 0))
    imag_side = jnp.where(first, roll(back_imag, -1, 0), roll(back_imag, 1, 0))
    message[:, 0, :] = back_real
    message[:, 1, :] = back_imag
    message[:, 2, :] = jnp.where(first | (row >= ROWS - 2), real_side, roll(imag_side, 8, 1))


def final_kernel(arrived, image_x, image_y, mix, turn, fine, out, push):
    side = arrived[:, 2, :]
    adjoint = jnp.concatenate(
        [
            jnp.concatenate([arrived[:, 0, :], side], 1),
            jnp.concatenate([arrived[:, 1, :], roll(side, -8, 1)], 1),
        ],
        0,
    ).astype(BF16)
    coarse = jnp.dot(mix[...], adjoint, preferred_element_type=F32)
    cos = turn[:, 0:128]
    sin = turn[:, 128:256]
    grads = []
    for lanes in (slice(0, 128), slice(128, 256)):
        real, imag = coarse[0:256, lanes], coarse[256:512, lanes]
        turned = jnp.concatenate([real * cos - imag * sin, real * sin + imag * cos], 1).astype(BF16)
        flat = lax.dot_general(fine[...], turned, NT, preferred_element_type=F32)
        grads.append(jnp.concatenate([flat[16 * i : 16 * i + 16, :] for i in range(8)], 1))
    own, near = grads
    push[0:2, :] = image_y[0:2, :] * near[14:16]
    push[2:18, :] = image_y[2:18, :] * own
    push[18:20, :] = image_y[18:20, :] * near[0:2]
    out[0] = -(col_slope(image_x[...] * own) + row_slope(push, ROWS))


def call(kernel, out_shape, scratch, *args):
    return pl.pallas_call(
        kernel,
        out_shape=out_shape,
        scratch_shapes=scratch,
        interpret=INTERPRET,
    )(*args)


def local(screens, image, vis_row, vis_block, vis_column, vis_real, vis_imag, vis_weight):
    shape = jax.ShapeDtypeStruct
    onward = [(i, (i + 1) % SLABS) for i in range(SLABS)]
    backward = [((i + 1) % SLABS, i) for i in range(SLABS)]
    fill = jnp.zeros((2, GRID), BF16)
    tail = jnp.concatenate([image[12:16].astype(BF16), screens[0, 14:16].astype(BF16), fill], 0)
    head = jnp.concatenate([image[0:4].astype(BF16), screens[0, 0:2].astype(BF16), fill], 0)
    above = lax.ppermute(tail, "slab", onward)
    below = lax.ppermute(head, "slab", backward)
    cells = jnp.stack(
        [
            vis_row.astype(F32),
            vis_block[:, 0].astype(F32),
            vis_column.astype(F32),
            vis_real,
            vis_imag,
            vis_weight,
            jnp.zeros_like(vis_real),
            jnp.zeros_like(vis_real),
        ]
    )
    bucket = call(bucket_kernel, shape((SLABS, 128), F32), [], cells)
    message, image_x, image_y = call(
        forward_kernel,
        (shape((SLABS, 3, 128), F32), shape((ROWS, GRID), F32), shape((24, GRID), F32)),
        [pltpu.VMEM((24, GRID), F32), pltpu.VMEM((24, GRID), F32), pltpu.VMEM((128, 512), BF16)],
        screens, image, above, below, bucket, table("row_mix"), table("row_turn"),
    )
    arrived = lax.all_to_all(message, "slab", 0, 0, tiled=True)
    message = call(
        middle_kernel, shape((SLABS, 3, 128), F32), [],
        arrived, table("col_mix"), table("col_turn"), table("fine_mix"), table("fine_mix_back"), table("col_mix_back"),
    )
    arrived = lax.all_to_all(message, "slab", 0, 0, tiled=True)
    return call(
        final_kernel, shape((1, ROWS, GRID), F32), [pltpu.VMEM((24, GRID), F32)],
        arrived, image_x, image_y, table("out_mix"), table("out_turn"), table("out_fine"),
    )


def solution(mesh):
    in_specs = (
        P(("chain", "vis"), "slab", None),
        P(("chain", "slab"), None),
        P("slab"),
        P("slab", None),
        P("slab"),
        P("slab"),
        P("slab"),
        P("slab"),
    )
    out_specs = P(("chain", "vis"), "slab", None)
    return jax.shard_map(local, mesh=mesh, in_specs=in_specs, out_specs=out_specs, check_vma=False)
```
